256 devices in a mesh: grp: 8 (over x, z_lo), ref: 32 (over z_hi, y, core).
Axes of the slice: x: 4, y: 4, z: 8 (z_hi: 4, z_lo: 2; z = z_hi * 2 + z_lo), core: 2. Of those that a mesh axis runs over, the one named last changes fastest.
Arguments:
- particles: bfloat16 [2048, 512], P(('grp', 'ref')), may hold values from -30 to 30
- samples: bfloat16 [131072, 512], P('ref'), may hold values from -6 to 6
Outputs:
- moved: float32 [2048, 512], P(('grp', 'ref'))
The draws below stay inside these ranges and needn't reach their ends.
All inputs are finite; a program needn't handle non-finite values.
Results may differ from the reference program's by a relative error of at most 0.0035.
Values may be sent and summed in bfloat16 or wider, within the bound.
A program may use at most 128 MiB of HBM per device.

```python
import jax
import jax.numpy as jnp
from jax import lax

D = 512
KERNEL_WIDTH = 16
PARTICLES = 2048
REFS = 131072


def draw_particles(key, part):
    values = jnp.clip(jax.random.normal(key, (PARTICLES, D), jnp.float32), -6.0, 6.0)
    return values.astype(jnp.bfloat16)


def steps_of(key, shape, split, low, top_value):
    def one(position, blocks):
        heights = jax.random.uniform(jax.random.fold_in(jax.random.fold_in(key, 6), position), (blocks,), jnp.float32, low / len(split), top_value / len(split))
        return jnp.repeat(jnp.exp(heights), shape[position] // blocks).reshape((-1,) + (1,) * (len(shape) - position - 1))

    level = one(*split[0])
    for cut in split[1:]:
        level = level * one(*cut)
    return level


def normal_values(rng, shape, width, bound, shards=(), kind=jnp.bfloat16):
    gain = steps_of(rng, shape, shards, -0.22, 0.18) if shards else 1.0
    result = jax.random.normal(rng, shape, jnp.float32) * width * gain
    return jnp.minimum(jnp.maximum(result, -bound), bound).astype(kind)


def setup_inputs(seed: int = 0) -> dict:
    arg_keys = jax.random.split(jax.random.key(seed), 3)
    return {
        "particles": draw_particles(jax.random.fold_in(arg_keys[2], 71), 0),
        "samples": normal_values(arg_keys[1], (REFS, D), 1.0, 6.0, ((0, 32),)),
    }


def square_norms(values):
    wide = values.astype(jnp.float32)
    return jnp.sum(wide * wide, axis=1)


def reference(particles, samples):
    step_size = 8.0
    masked_score = -1.0e30
    block_rows = min(256, PARTICLES)
    blocks = PARTICLES // block_rows
    part_sq = square_norms(particles)
    ref_sq = square_norms(samples)
    all_ids = jnp.arange(PARTICLES, dtype=jnp.int32)

    def one_block(inputs):
        row_block, row_sq, row_ids = inputs
        cross_scores = (2.0 * jnp.dot(row_block, samples.T, preferred_element_type=jnp.float32) - row_sq[:, None] - ref_sq[None, :]) / (2.0 * KERNEL_WIDTH)
        cross_top = jnp.max(cross_scores, axis=1)
        cross_weights = jnp.exp(cross_scores - cross_top[:, None])
        cross_total = jnp.sum(cross_weights, axis=1)
        cross_mean = jnp.dot(cross_weights.astype(jnp.bfloat16), samples, preferred_element_type=jnp.float32) / cross_total[:, None]
        self_scores = (2.0 * jnp.dot(row_block, particles.T, preferred_element_type=jnp.float32) - row_sq[:, None] - part_sq[None, :]) / (2.0 * KERNEL_WIDTH)
        diag_mask = row_ids[:, None] == all_ids[None, :]
        self_scores = jnp.where(diag_mask, masked_score, self_scores)
        self_top = jnp.max(self_scores, axis=1)
        self_weights = jnp.where(diag_mask, 0.0, jnp.exp(self_scores - self_top[:, None]))
        self_total = jnp.sum(self_weights, axis=1)
        self_mean = jnp.dot(self_weights.astype(jnp.bfloat16), particles, preferred_element_type=jnp.float32) / self_total[:, None]
        return row_block.astype(jnp.float32) + step_size * (cross_mean - self_mean)

    moved = lax.map(one_block, (particles.reshape(blocks, block_rows, D), part_sq.reshape(blocks, block_rows), all_ids.reshape(blocks, block_rows)))
    return moved.reshape(PARTICLES, D)
```

```python
import functools
import math

import jax
import jax.numpy as jnp
from jax import lax
from jax.experimental import pallas as pl
from jax.experimental.pallas import tpu as pltpu
from jax.sharding import PartitionSpec as P

KERNEL_WIDTH = 16
STEP_SIZE = 8.0
MASKED = -1e30
SCALE = math.log2(math.e) / (2.0 * KERNEL_WIDTH)
MESH = pl.DeviceIdType.MESH
CHUNK = 512
LANES = 128


def split3(value):
    hi = value.astype(jnp.bfloat16).astype(jnp.float32)
    mid = (value - hi).astype(jnp.bfloat16).astype(jnp.float32)
    return hi, mid, value - hi - mid


def with_stats(total, top, mass):
    lane = lax.broadcasted_iota(jnp.int32, (total.shape[0], LANES), 1)
    stats = jnp.zeros((total.shape[0], LANES), jnp.float32)
    for at, piece in enumerate(split3(top) + split3(mass)):
        stats = jnp.where(lane == at, piece, stats)
    return jnp.concatenate([total, stats], axis=1)


def merged_mean(parts):
    wide = parts.astype(jnp.float32)
    d = wide.shape[2] - LANES
    top = wide[:, :, d : d + 1] + wide[:, :, d + 1 : d + 2] + wide[:, :, d + 2 : d + 3]
    mass = wide[:, :, d + 3 : d + 4] + wide[:, :, d + 4 : d + 5] + wide[:, :, d + 5 : d + 6]
    share = jnp.exp2(top - jnp.max(top, axis=0, keepdims=True))
    return jnp.sum(share * wide[:, :, :d], axis=0) / jnp.sum(share * mass, axis=0)


def lane_square_norms(values):
    n, d = values.shape
    wide = values.astype(jnp.float32)
    wide = wide * wide
    part = wide[:, :LANES]
    for at in range(LANES, d, LANES):
        part = part + wide[:, at : at + LANES]
    return jnp.sum(part.T, axis=0, keepdims=True)


def kernel(
    p_ref, samples_ref, out_ref,
    smp, rows, cols, pmat, ref_sq, scores, acc, send_c, recv_c, send_s, recv_s,
    load_sem, gs_sem, gr_sem, cs_sem, cr_sem, ss_sem, sr_sem,
):
    n_ref, n_grp = lax.axis_size("ref"), lax.axis_size("grp")
    me, mine = lax.axis_index("ref"), lax.axis_index("grp")
    part, d = p_ref.shape
    n_rows = n_ref * part
    chunks = smp.shape[0]

    def load(j):
        return pltpu.make_async_copy(
            samples_ref.at[pl.ds(j * CHUNK, CHUNK)], smp.at[j], load_sem.at[j]
        )

    for j in range(chunks):
        load(j).start()

    barrier = pltpu.get_barrier_semaphore()

    def greet_ref(k, c):
        pl.semaphore_signal(barrier, inc=1, device_id={"ref": lax.rem(me + k, n_ref)}, device_id_type=MESH)
        return c

    def greet_grp(k, c):
        pl.semaphore_signal(barrier, inc=1, device_id={"grp": lax.rem(mine + k, n_grp)}, device_id_type=MESH)
        return c

    lax.fori_loop(1, n_ref, greet_ref, 0)
    lax.fori_loop(1, n_grp, greet_grp, 0)
    rows[me] = p_ref[...]
    cols[mine] = p_ref[...]

    def square(j, c):
        load(j).wait()
        ref_sq[j] = lane_square_norms(smp[j]) * SCALE
        return c

    lax.fori_loop(0, chunks, square, 0)
    pl.semaphore_wait(barrier, n_ref - 1 + n_grp - 1)

    def give_row(k, c):
        pltpu.make_async_remote_copy(
            p_ref, rows.at[me], gs_sem.at[0], gr_sem.at[0],
            device_id={"ref": lax.rem(me + k, n_ref)}, device_id_type=MESH,
        ).start()
        return c

    def give_col(k, c):
        pltpu.make_async_remote_copy(
            p_ref, cols.at[mine], gs_sem.at[1], gr_sem.at[1],
            device_id={"grp": lax.rem(mine + k, n_grp)}, device_id_type=MESH,
        ).start()
        return c

    lax.fori_loop(1, n_ref, give_row, 0)
    lax.fori_loop(1, n_grp, give_col, 0)

    def all_of(buf, n, send_sem, recv_sem):
        return pltpu.make_async_remote_copy(
            buf.at[pl.ds(0, n - 1)], buf.at[pl.ds(0, n - 1)], send_sem, recv_sem,
            device_id={"ref": lax.rem(me + 1, n_ref)}, device_id_type=MESH,
        )

    got_rows = all_of(rows, n_ref, gs_sem.at[0], gr_sem.at[0])
    got_cols = all_of(cols, n_grp, gs_sem.at[1], gr_sem.at[1])
    got_rows.wait_recv()
    wide = rows[...].astype(jnp.float32).reshape(n_rows, d)
    pmat[...] = wide.astype(jnp.bfloat16)
    row_sq = jnp.sum(wide * wide, axis=1, keepdims=True) * SCALE

    got_cols.wait_recv()
    cmat = cols[...].astype(jnp.float32).reshape(n_grp * part, d).astype(jnp.bfloat16)
    col_sq = lane_square_norms(cmat) * SCALE
    n_cols = n_grp * part
    s = lax.dot_general(pmat[...], cmat, (((1,), (1,)), ((), ())), preferred_element_type=jnp.float32)
    s = s * (2.0 * SCALE) - col_sq
    row_id = mine * n_rows + lax.broadcasted_iota(jnp.int32, (n_rows, n_cols), 0)
    at = lax.broadcasted_iota(jnp.int32, (n_rows, n_cols), 1)
    col_id = (at // part) * n_rows + me * part + at % part
    same = row_id == col_id
    s = jnp.where(same, MASKED, s)
    s_top = jnp.max(s, axis=1, keepdims=True)
    w = jnp.where(same, 0.0, jnp.exp2(s - s_top))
    s_mass = jnp.sum(w, axis=1, keepdims=True)
    s_sum = jnp.dot(w.astype(jnp.bfloat16), cmat, preferred_element_type=jnp.float32)
    send_s[...] = with_stats(s_sum, s_top - row_sq, s_mass).reshape(n_ref, part, d + LANES).astype(jnp.bfloat16)

    def give(send, recv, send_sem, recv_sem):
        def one(k, c):
            peer = lax.rem(me + k, n_ref)
            pltpu.make_async_remote_copy(
                send.at[peer], recv.at[me], send_sem, recv_sem,
                device_id={"ref": peer}, device_id_type=MESH,
            ).start()
            return c

        lax.fori_loop(1, n_ref, one, 0)
        recv[me] = send[me]

    give(send_s, recv_s, ss_sem, sr_sem)

    def score(j, top):
        s = lax.dot_general(
            pmat[...], smp[j], (((1,), (1,)), ((), ())), preferred_element_type=jnp.float32
        )
        s = s * (2.0 * SCALE) - ref_sq[j]
        scores[j] = s
        for a in range(0, CHUNK, LANES):
            top = jnp.maximum(top, s[:, a : a + LANES])
        return top

    top = lax.fori_loop(0, chunks, score, jnp.full((n_rows, LANES), -jnp.inf, jnp.float32))
    top = jnp.max(top, axis=1, keepdims=True)
    acc[...] = jnp.zeros_like(acc)

    def weigh(j, mass):
        w = jnp.exp2(scores[j] - top)
        for a in range(0, CHUNK, LANES):
            mass = mass + w[:, a : a + LANES]
        acc[...] += jnp.dot(w.astype(jnp.bfloat16), smp[j], preferred_element_type=jnp.float32)
        return mass

    mass = lax.fori_loop(0, chunks, weigh, jnp.zeros((n_rows, LANES), jnp.float32))
    mass = jnp.sum(mass, axis=1, keepdims=True)
    send_c[...] = with_stats(acc[...], top - row_sq, mass).reshape(n_ref, part, d + LANES).astype(jnp.bfloat16)
    give(send_c, recv_c, cs_sem, cr_sem)

    got_s = all_of(recv_s, n_ref, ss_sem, sr_sem)
    got_c = all_of(recv_c, n_ref, cs_sem, cr_sem)
    got_s.wait_recv()
    self_mean = merged_mean(recv_s[...])
    got_c.wait_recv()
    cross_mean = merged_mean(recv_c[...])
    out_ref[...] = p_ref[...].astype(jnp.float32) + STEP_SIZE * (cross_mean - self_mean)
    got_rows.wait_send()
    got_cols.wait_send()
    got_s.wait_send()
    got_c.wait_send()


def per_device(n_ref, n_grp, particles, samples):
    part, d = particles.shape
    refs = samples.shape[0]
    n_rows, chunks = n_ref * part, refs // CHUNK
    dma = pltpu.SemaphoreType.DMA
    bf16, f32 = jnp.bfloat16, jnp.float32
    return pl.pallas_call(
        kernel,
        out_shape=jax.ShapeDtypeStruct((part, d), f32),
        in_specs=[pl.BlockSpec(memory_space=pltpu.VMEM), pl.BlockSpec(memory_space=pl.ANY)],
        out_specs=pl.BlockSpec(memory_space=pltpu.VMEM),
        scratch_shapes=[
            pltpu.VMEM((chunks, CHUNK, d), bf16),
            pltpu.VMEM((n_ref, part, d), bf16),
            pltpu.VMEM((n_grp, part, d), bf16),
            pltpu.VMEM((n_rows, d), bf16),
            pltpu.VMEM((chunks, 1, CHUNK), f32),
            pltpu.VMEM((chunks, n_rows, CHUNK), f32),
            pltpu.VMEM((n_rows, d), f32),
            pltpu.VMEM((n_ref, part, d + LANES), bf16),
            pltpu.VMEM((n_ref, part, d + LANES), bf16),
            pltpu.VMEM((n_ref, part, d + LANES), bf16),
            pltpu.VMEM((n_ref, part, d + LANES), bf16),
            dma((chunks,)), dma((2,)), dma((2,)), dma, dma, dma, dma,
        ],
        compiler_params=pltpu.CompilerParams(
            collective_id=0, has_side_effects=True, vmem_limit_bytes=56 * 2**20
        ),
        name="mmd_step",
    )(particles, samples)


def solution(mesh):
    step = functools.partial(per_device, mesh.shape["ref"], mesh.shape["grp"])
    return jax.shard_map(
        step,
        mesh=mesh,
        in_specs=(P(("grp", "ref"), None), P("ref", None)),
        out_specs=P(("grp", "ref"), None),
        check_vma=False,
    )
```

```python
import functools
import math

import jax
import jax.numpy as jnp
from jax import lax
from jax.experimental import pallas as pl
from jax.experimental.pallas import tpu as pltpu
from jax.sharding import PartitionSpec as P

KERNEL_WIDTH = 16
STEP_SIZE = 8.0
MASKED = -1e30
SCALE = math.log2(math.e) / (2.0 * KERNEL_WIDTH)
MESH = pl.DeviceIdType.MESH
CHUNK = 512
LANES = 128
VMEM_BYTES = 56 * 2**20
Z, Y = 4, 4


def split3(value):
    hi = value.astype(jnp.bfloat16).astype(jnp.float32)
    mid = (value - hi).astype(jnp.bfloat16).astype(jnp.float32)
    return hi, mid, value - hi - mid


def stats_lanes(*columns):
    lane = lax.broadcasted_iota(jnp.int32, (columns[0].shape[0], LANES), 1)
    stats = jnp.zeros((columns[0].shape[0], LANES), jnp.float32)
    for n, column in enumerate(columns):
        for m, piece in enumerate(split3(column)):
            stats = jnp.where(lane == 3 * n + m, piece, stats)
    return stats


def stat(stats, n):
    return stats[..., 3 * n : 3 * n + 1] + stats[..., 3 * n + 1 : 3 * n + 2] + stats[..., 3 * n + 2 : 3 * n + 3]


def merged_mean(parts, top, mass):
    share = jnp.exp2(top - jnp.max(top, axis=0, keepdims=True))
    return jnp.sum(share * parts, axis=0) / jnp.sum(share * mass, axis=0)


def lane_square_norms(values):
    n, d = values.shape
    wide = values.astype(jnp.float32)
    wide = wide * wide
    part = wide[:, :LANES]
    for at in range(LANES, d, LANES):
        part = part + wide[:, at : at + LANES]
    return jnp.sum(part.T, axis=0, keepdims=True)


def dot_nt(a, b):
    return lax.dot_general(a, b, (((1,), (1,)), ((), ())), preferred_element_type=jnp.float32)


def kernel(
    p_hbm, samples_ref, out_ref,
    p_ref, smp, rows, cols, pmat, ref_sq, scores, acc,
    send_m, recv_m, send_c, recv_c, send_s, recv_s,
    load_sem, p_sem, row_send, row_recv, col_send, col_recv, fwd_send, fwd_recv, fwc_send, fwc_recv,
    m_send, m_recv, c_send, c_recv, s_send, s_recv,
):
    n_grp = lax.axis_size("grp")
    me, mine = lax.axis_index("ref"), lax.axis_index("grp")
    core, y, zh = me % 2, (me // 2) % Y, me // (2 * Y)
    mate = me + 1 - 2 * core
    part, d = p_ref.shape
    chips = Z * Y
    half = chips * part
    chunks = smp.shape[0]
    far_first = [(a, b) for a in (2, 1, 3, 0) for b in (2, 1, 3, 0) if (a, b) != (0, 0)]

    def ahead(a, b):
        return (((zh + a) % Z) * Y + (y + b) % Y) * 2 + core

    def behind(a, b):
        return (((zh + Z - a) % Z) * Y + (y + Y - b) % Y) * 2 + core

    def remote(src, dst, send_sem, recv_sem, **where):
        return pltpu.make_async_remote_copy(
            src, dst, send_sem, recv_sem, device_id=where, device_id_type=MESH
        )

    barrier = pltpu.get_barrier_semaphore()
    for a, b in far_first:
        pl.semaphore_signal(barrier, inc=1, device_id={"ref": behind(a, b)}, device_id_type=MESH)
    for j in range(1, n_grp):
        pl.semaphore_signal(barrier, inc=1, device_id={"grp": (mine + j) % n_grp}, device_id_type=MESH)
    pl.semaphore_signal(barrier, inc=1, device_id={"ref": mate}, device_id_type=MESH)

    load_p = pltpu.make_async_copy(p_hbm, p_ref, p_sem)
    load_p.start()

    def load(j):
        return pltpu.make_async_copy(
            samples_ref.at[pl.ds(j * CHUNK, CHUNK)], smp.at[j], load_sem.at[j]
        )

    for j in range(chunks):
        load(j).start()

    load_p.wait()
    rows[0] = p_ref[...]
    cols[0] = p_ref[...]

    def square(j, c):
        load(j).wait()
        ref_sq[j] = lane_square_norms(smp[j]) * SCALE
        return c

    lax.fori_loop(0, chunks, square, 0)
    pl.semaphore_wait(barrier, chips - 1 + n_grp - 1 + 1)

    for a, b in far_first:
        remote(p_ref, rows.at[a * Y + b], row_send, row_recv.at[a], ref=ahead(a, b)).start()
    for j in range(1, n_grp):
        remote(p_ref, cols.at[j], col_send, col_recv, grp=(mine + j) % n_grp).start()

    def slots(buf, start, n, send_sem, recv_sem):
        return remote(buf.at[pl.ds(start, n)], buf.at[pl.ds(start, n)], send_sem, recv_sem, ref=mate)

    for a in (0, 1, 3, 2):
        n = Y - 1 if a == 0 else Y
        slots(rows, 0, n, row_send, row_recv.at[a]).wait_recv()
        remote(rows.at[pl.ds(a * Y, Y)], rows.at[pl.ds(chips + a * Y, Y)], fwd_send, fwd_recv, ref=mate).start()
        if a == 0:
            slots(cols, 0, n_grp - 1, col_send, col_recv).wait_recv()
            remote(cols.at[pl.ds(0, n_grp)], cols.at[pl.ds(n_grp, n_grp)], fwc_send, fwc_recv, ref=mate).start()
    forward_cols = slots(cols, n_grp, n_grp, fwc_send, fwc_recv)
    forward_cols.wait_recv()

    cwide = cols[...].astype(jnp.float32).reshape(2 * n_grp * part, d)
    cmat = cwide.astype(jnp.bfloat16)
    col_sq = lane_square_norms(cmat) * SCALE
    n_cols = 2 * n_grp * part

    forward_rows = slots(rows, chips, chips, fwd_send, fwd_recv)
    forward_rows.wait_recv()
    wide = rows[...].astype(jnp.float32).reshape(2 * half, d)
    pmat[...] = wide.astype(jnp.bfloat16)
    row_sq = jnp.sum(wide * wide, axis=1, keepdims=True) * SCALE
    center = jnp.sum(wide, axis=0, keepdims=True) * (1.0 / (2 * half))

    s = dot_nt(pmat[pl.ds(0, half), :], cmat)
    s = s * (2.0 * SCALE) - col_sq
    r = lax.broadcasted_iota(jnp.int32, (half, n_cols), 0)
    a, b = r // (Y * part), (r // part) % Y
    row_id = mine * (2 * half) + (((zh + Z - a) % Z * Y + (y + Y - b) % Y) * 2 + core) * part + r % part
    q = lax.broadcasted_iota(jnp.int32, (half, n_cols), 1)
    j = (q // part) % n_grp
    col_id = (
        (mine + n_grp - j) % n_grp * (2 * half)
        + jnp.where(q < n_grp * part, me, mate) * part
        + q % part
    )
    same = row_id == col_id
    s = jnp.where(same, MASKED, s)
    s_top = jnp.max(s, axis=1, keepdims=True)
    w = jnp.where(same, 0.0, jnp.exp2(s - s_top))
    s_mass = jnp.sum(w, axis=1, keepdims=True)
    s_sum = jnp.dot(w.astype(jnp.bfloat16), cmat, preferred_element_type=jnp.float32) - s_mass * center
    send_s[...] = s_sum.reshape(chips, part, d).astype(jnp.bfloat16)

    for a, b in far_first:
        k = a * Y + b
        remote(send_s.at[k], recv_s.at[k], s_send, s_recv, ref=behind(a, b)).start()
    recv_s[0] = send_s[0]

    top = jnp.full((2 * half, LANES), -jnp.inf, jnp.float32)
    for j in range(chunks):
        s = dot_nt(pmat[...], smp[j]) * (2.0 * SCALE) - ref_sq[j]
        scores[j] = s
        for at in range(0, CHUNK, LANES):
            top = jnp.maximum(top, s[:, at : at + LANES])
    top = jnp.max(top, axis=1, keepdims=True)
    mass = jnp.zeros((2 * half, LANES), jnp.float32)
    for j in range(chunks):
        w = jnp.exp2(scores[j] - top)
        for at in range(0, CHUNK, LANES):
            mass = mass + w[:, at : at + LANES]
        term = jnp.dot(w.astype(jnp.bfloat16), smp[j], preferred_element_type=jnp.float32)
        if j == 0:
            acc[...] = term
        else:
            acc[...] += term
    mass = jnp.sum(mass, axis=1, keepdims=True)
    total = acc[...] - mass * center
    top = top - row_sq

    send_m[:, pl.ds(0, d)] = total[half:].astype(jnp.bfloat16)
    send_m[:, pl.ds(d, LANES)] = stats_lanes(top[half:], mass[half:]).astype(jnp.bfloat16)
    swap = remote(send_m, recv_m, m_send, m_recv, ref=mate)
    swap.start()
    swap.wait_recv()
    theirs = recv_m[:, pl.ds(0, d)].astype(jnp.float32)
    stats = recv_m[:, pl.ds(d, LANES)].astype(jnp.float32)
    c_top = jnp.maximum(top[:half], stat(stats, 0))
    ours_share, their_share = jnp.exp2(top[:half] - c_top), jnp.exp2(stat(stats, 0) - c_top)
    c_mass = mass[:half] * ours_share + stat(stats, 1) * their_share
    c_sum = total[:half] * ours_share + theirs * their_share
    send_c[:, :, pl.ds(0, d)] = c_sum.reshape(chips, part, d).astype(jnp.bfloat16)
    stats = stats_lanes(c_top, c_mass, s_top - row_sq[:half], s_mass)
    send_c[:, :, pl.ds(d, LANES)] = stats.reshape(chips, part, LANES).astype(jnp.bfloat16)

    for a, b in far_first:
        k = a * Y + b
        remote(send_c.at[k], recv_c.at[k], c_send, c_recv, ref=behind(a, b)).start()
    recv_c[0] = send_c[0]

    got_s = slots(recv_s, 0, chips - 1, s_send, s_recv)
    got_c = slots(recv_c, 0, chips - 1, c_send, c_recv)
    got_s.wait_recv()
    got_c.wait_recv()
    stats = recv_c[:, :, pl.ds(d, LANES)].astype(jnp.float32)
    cross = merged_mean(recv_c[:, :, pl.ds(0, d)].astype(jnp.float32), stat(stats, 0), stat(stats, 1))
    own = merged_mean(recv_s[...].astype(jnp.float32), stat(stats, 2), stat(stats, 3))
    out_ref[...] = p_ref[...].astype(jnp.float32) + STEP_SIZE * (cross - own)
    slots(rows, 0, chips - 1, row_send, row_recv.at[0]).wait_send()
    slots(cols, 0, n_grp - 1, col_send, col_recv).wait_send()
    forward_rows.wait_send()
    forward_cols.wait_send()
    swap.wait_send()
    got_s.wait_send()
    got_c.wait_send()


def per_device(n_ref, n_grp, particles, samples):
    part, d = particles.shape
    refs = samples.shape[0]
    chips, chunks = n_ref // 2, refs // CHUNK
    n_rows, half = n_ref * part, n_ref * part // 2
    dma = pltpu.SemaphoreType.DMA
    bf16, f32 = jnp.bfloat16, jnp.float32
    return pl.pallas_call(
        kernel,
        out_shape=jax.ShapeDtypeStruct((part, d), f32),
        in_specs=[pl.BlockSpec(memory_space=pl.ANY)] * 2,
        out_specs=pl.BlockSpec(memory_space=pltpu.VMEM),
        scratch_shapes=[
            pltpu.VMEM((part, d), bf16),
            pltpu.VMEM((chunks, CHUNK, d), bf16),
            pltpu.VMEM((n_ref, part, d), bf16),
            pltpu.VMEM((2 * n_grp, part, d), bf16),
            pltpu.VMEM((n_rows, d), bf16),
            pltpu.VMEM((chunks, 1, CHUNK), f32),
            pltpu.VMEM((chunks, n_rows, CHUNK), f32),
            pltpu.VMEM((n_rows, d), f32),
            pltpu.VMEM((half, d + LANES), bf16),
            pltpu.VMEM((half, d + LANES), bf16),
            pltpu.VMEM((chips, part, d + LANES), bf16),
            pltpu.VMEM((chips, part, d + LANES), bf16),
            pltpu.VMEM((chips, part, d), bf16),
            pltpu.VMEM((chips, part, d), bf16),
            dma((chunks,)), dma, dma, dma((Z,)), dma, dma, dma, dma, dma, dma,
            dma, dma, dma, dma, dma, dma,
        ],
        compiler_params=pltpu.CompilerParams(
            collective_id=0, has_side_effects=True, vmem_limit_bytes=VMEM_BYTES
        ),
        name="mmd_step",
    )(particles, samples)


def solution(mesh):
    step = functools.partial(per_device, mesh.shape["ref"], mesh.shape["grp"])
    return jax.shard_map(
        step,
        mesh=mesh,
        in_specs=(P(("grp", "ref"), None), P("ref", None)),
        out_specs=P(("grp", "ref"), None),
        check_vma=False,
    )
```

```python
import functools
import math

import jax
import jax.numpy as jnp
from jax import lax
from jax.experimental import pallas as pl
from jax.experimental.pallas import tpu as pltpu
from jax.sharding import PartitionSpec as P

KERNEL_WIDTH = 16
STEP_SIZE = 8.0
MASKED = -1e30
SCALE = math.log2(math.e) / (2.0 * KERNEL_WIDTH)
MESH = pl.DeviceIdType.MESH
CHUNK = 512
LANES = 128
VMEM_BYTES = 56 * 2**20
Z, Y, LO = 4, 4, 2


def split3(value):
    hi = value.astype(jnp.bfloat16).astype(jnp.float32)
    mid = (value - hi).astype(jnp.bfloat16).astype(jnp.float32)
    return hi, mid, value - hi - mid


def stats_lanes(*columns):
    lane = lax.broadcasted_iota(jnp.int32, (columns[0].shape[0], LANES), 1)
    stats = jnp.zeros((columns[0].shape[0], LANES), jnp.float32)
    for n, column in enumerate(columns):
        for m, piece in enumerate(split3(column)):
            stats = jnp.where(lane == 3 * n + m, piece, stats)
    return stats


def stat(stats, n):
    return stats[..., 3 * n : 3 * n + 1] + stats[..., 3 * n + 1 : 3 * n + 2] + stats[..., 3 * n + 2 : 3 * n + 3]


def merged_mean(parts, top, mass):
    share = jnp.exp2(top - jnp.max(top, axis=0, keepdims=True))
    return jnp.sum(share * parts, axis=0) / jnp.sum(share * mass, axis=0)


def lane_square_norms(values):
    n, d = values.shape
    wide = values.astype(jnp.float32)
    wide = wide * wide
    part = wide[:, :LANES]
    for at in range(LANES, d, LANES):
        part = part + wide[:, at : at + LANES]
    return jnp.sum(part.T, axis=0, keepdims=True)


def dot_nt(a, b):
    return lax.dot_general(a, b, (((1,), (1,)), ((), ())), preferred_element_type=jnp.float32)


def kernel(
    p_hbm, samples_ref, out_ref,
    p_ref, smp, rows, cols, pmat, ref_sq, scores, acc,
    send_m, recv_m, send_c, recv_c, send_s, recv_s,
    load_sem, p_sem, row_send, row_recv, col_send, col_recv, fwd_send, fwd_recv, fwc_send, fwc_recv,
    m_send, m_recv, c_send, c_recv, s_send, s_recv,
):
    n_grp = lax.axis_size("grp")
    me, mine = lax.axis_index("ref"), lax.axis_index("grp")
    core, y, zh = me % 2, (me // 2) % Y, me // (2 * Y)
    mate = me + 1 - 2 * core
    part, d = p_ref.shape
    chips = Z * Y
    half = chips * part
    chunks = smp.shape[0]
    far_first = [(a, b) for a in (2, 1, 3, 0) for b in (2, 1, 3, 0) if (a, b) != (0, 0)]

    lo, x = mine % LO, mine // LO

    def goes_to(a, b):
        to_lo = (lo, 0, 1 - lo, 1)[a]
        where = {"grp": x * LO + to_lo, "ref": (((zh + a) % Z) * Y + (y + b) % Y) * 2 + core}
        return where, (0, 1 + 2 * lo, 2, 1 + 2 * lo)[a] * Y + b

    def z_of_slot(s):
        if s == 0:
            return zh, lo
        if s == 2:
            return (zh + 2) % Z, 1 - lo
        return (zh + Z - 1 + 2 * lo) % Z, s // 2

    def comes_from(s, b):
        from_zh, from_lo = z_of_slot(s)
        return {"grp": x * LO + from_lo, "ref": (from_zh * Y + (y + Y - b) % Y) * 2 + core}

    def returns_to(s, b):
        return comes_from(s, b), (0, 1 + 2 * lo, 2, 1 + 2 * lo)[s] * Y + b

    def remote(src, dst, send_sem, recv_sem, **where):
        return pltpu.make_async_remote_copy(
            src, dst, send_sem, recv_sem, device_id=where, device_id_type=MESH
        )

    barrier = pltpu.get_barrier_semaphore()
    for a, b in far_first:
        pl.semaphore_signal(barrier, inc=1, device_id=comes_from(a, b), device_id_type=MESH)
    for j in range(1, n_grp):
        pl.semaphore_signal(barrier, inc=1, device_id={"grp": (mine + j) % n_grp}, device_id_type=MESH)
    pl.semaphore_signal(barrier, inc=1, device_id={"ref": mate}, device_id_type=MESH)

    load_p = pltpu.make_async_copy(p_hbm, p_ref, p_sem)
    load_p.start()

    def load(j):
        return pltpu.make_async_copy(
            samples_ref.at[pl.ds(j * CHUNK, CHUNK)], smp.at[j], load_sem.at[j]
        )

    for j in range(chunks):
        load(j).start()

    load_p.wait()
    rows[0] = p_ref[...]
    cols[0] = p_ref[...]

    def square(j, c):
        load(j).wait()
        ref_sq[j] = lane_square_norms(smp[j]) * SCALE
        return c

    lax.fori_loop(0, chunks, square, 0)
    pl.semaphore_wait(barrier, chips - 1 + n_grp - 1 + 1)

    for a, b in far_first:
        where, slot = goes_to(a, b)
        remote(p_ref, rows.at[slot], row_send, row_recv.at[slot // Y], **where).start()
    for j in range(1, n_grp):
        remote(p_ref, cols.at[j], col_send, col_recv, grp=(mine + j) % n_grp).start()

    def slots(buf, start, n, send_sem, recv_sem):
        return remote(buf.at[pl.ds(start, n)], buf.at[pl.ds(start, n)], send_sem, recv_sem, ref=mate)

    for a in (0, 1, 3, 2):
        n = Y - 1 if a == 0 else Y
        slots(rows, 0, n, row_send, row_recv.at[a]).wait_recv()
        remote(rows.at[pl.ds(a * Y, Y)], rows.at[pl.ds(chips + a * Y, Y)], fwd_send, fwd_recv, ref=mate).start()
    forward_rows = slots(rows, chips, chips, fwd_send, fwd_recv)
    slots(cols, 0, n_grp - 1, col_send, col_recv).wait_recv()
    remote(cols.at[pl.ds(0, n_grp)], cols.at[pl.ds(n_grp, n_grp)], fwc_send, fwc_recv, ref=mate).start()
    forward_cols = slots(cols, n_grp, n_grp, fwc_send, fwc_recv)

    def prepare(start):
        wide = rows[pl.ds(start, chips)].astype(jnp.float32).reshape(half, d)
        pmat[pl.ds(start * part, half), :] = wide.astype(jnp.bfloat16)
        square = jnp.sum(wide * wide, axis=1, keepdims=True)
        n = Y * part
        mean = jnp.sum(wide.reshape(Z, n, d), axis=1, keepdims=True) * (1.0 / n)
        of_mean = jnp.sum(mean * mean, axis=2, keepdims=True)
        of_rows = jnp.sum(square.reshape(Z, n, 1), axis=1, keepdims=True) * (1.0 / n)
        noise = (of_rows - of_mean) * (1.0 / (n - 1))
        return square * SCALE, mean * jnp.maximum(1.0 - noise / jnp.maximum(of_mean, 1e-30), 0.0)

    def less_center(total, mass, center):
        parted = total.reshape(Z, Y * part, d) - mass.reshape(Z, Y * part, 1) * center
        return parted.reshape(half, d)

    own_sq, own_center = prepare(0)
    forward_cols.wait_recv()
    cmat = cols[...].astype(jnp.float32).reshape(2 * n_grp * part, d).astype(jnp.bfloat16)
    col_sq = lane_square_norms(cmat) * SCALE
    n_cols = 2 * n_grp * part

    s = dot_nt(pmat[pl.ds(0, half), :], cmat)
    s = s * (2.0 * SCALE) - col_sq
    r = lax.broadcasted_iota(jnp.int32, (half, 1), 0)
    a, b = r // (Y * part), (r // part) % Y
    row_base = jnp.zeros((half, 1), jnp.int32)
    for n in range(Z):
        from_zh, from_lo = z_of_slot(n)
        base = (x * LO + from_lo) * (2 * half) + (from_zh * Y * 2 + core) * part
        row_base = jnp.where(a == n, base, row_base)
    row_id = row_base + ((y + Y - b) % Y) * (2 * part) + r % part
    q = lax.broadcasted_iota(jnp.int32, (1, n_cols), 1)
    j = (q // part) % n_grp
    col_id = (
        (mine + n_grp - j) % n_grp * (2 * half)
        + jnp.where(q < n_grp * part, me, mate) * part
        + q % part
    )
    same = row_id == col_id
    s = jnp.where(same, MASKED, s)
    s_top = jnp.max(s, axis=1, keepdims=True)
    w = jnp.where(same, 0.0, jnp.exp2(s - s_top))
    s_mass = jnp.sum(w, axis=1, keepdims=True)
    s_sum = jnp.dot(w.astype(jnp.bfloat16), cmat, preferred_element_type=jnp.float32)
    send_s[...] = less_center(s_sum, s_mass, own_center).reshape(chips, part, d).astype(jnp.bfloat16)

    for a, b in far_first:
        where, slot = returns_to(a, b)
        remote(send_s.at[a * Y + b], recv_s.at[slot], s_send, s_recv, **where).start()
    recv_s[0] = send_s[0]

    forward_rows.wait_recv()
    other_sq, other_center = prepare(chips)

    top = jnp.full((2 * half, LANES), -jnp.inf, jnp.float32)
    for j in range(chunks):
        s = dot_nt(pmat[...], smp[j]) * (2.0 * SCALE) - ref_sq[j]
        scores[j] = s
        for at in range(0, CHUNK, LANES):
            top = jnp.maximum(top, s[:, at : at + LANES])
    top = jnp.max(top, axis=1, keepdims=True)
    mass = jnp.zeros((2 * half, LANES), jnp.float32)
    for j in range(chunks):
        w = jnp.exp2(scores[j] - top)
        for at in range(0, CHUNK, LANES):
            mass = mass + w[:, at : at + LANES]
        term = jnp.dot(w.astype(jnp.bfloat16), smp[j], preferred_element_type=jnp.float32)
        if j == 0:
            acc[...] = term
        else:
            acc[...] += term
    mass = jnp.sum(mass, axis=1, keepdims=True)
    own_mass, other_mass = mass[:half], mass[half:]
    own_top, other_top = top[:half] - own_sq, top[half:] - other_sq
    own_total = less_center(acc[pl.ds(0, half), :], own_mass, own_center)
    other_total = less_center(acc[pl.ds(half, half), :], other_mass, other_center)

    send_m[:, pl.ds(0, d)] = other_total.astype(jnp.bfloat16)
    send_m[:, pl.ds(d, LANES)] = stats_lanes(other_top, other_mass).astype(jnp.bfloat16)
    swap = remote(send_m, recv_m, m_send, m_recv, ref=mate)
    swap.start()
    swap.wait_recv()
    theirs = recv_m[:, pl.ds(0, d)].astype(jnp.float32)
    stats = recv_m[:, pl.ds(d, LANES)].astype(jnp.float32)
    c_top = jnp.maximum(own_top, stat(stats, 0))
    ours_share, their_share = jnp.exp2(own_top - c_top), jnp.exp2(stat(stats, 0) - c_top)
    c_mass = own_mass * ours_share + stat(stats, 1) * their_share
    c_sum = own_total * ours_share + theirs * their_share
    send_c[:, :, pl.ds(0, d)] = c_sum.reshape(chips, part, d).astype(jnp.bfloat16)
    stats = stats_lanes(c_top, c_mass, s_top - own_sq, s_mass)
    send_c[:, :, pl.ds(d, LANES)] = stats.reshape(chips, part, LANES).astype(jnp.bfloat16)

    for a, b in far_first:
        where, slot = returns_to(a, b)
        remote(send_c.at[a * Y + b], recv_c.at[slot], c_send, c_recv, **where).start()
    recv_c[0] = send_c[0]

    got_s = slots(recv_s, 0, chips - 1, s_send, s_recv)
    got_c = slots(recv_c, 0, chips - 1, c_send, c_recv)
    got_s.wait_recv()
    got_c.wait_recv()
    stats = recv_c[:, :, pl.ds(d, LANES)].astype(jnp.float32)
    cross = merged_mean(recv_c[:, :, pl.ds(0, d)].astype(jnp.float32), stat(stats, 0), stat(stats, 1))
    own = merged_mean(recv_s[...].astype(jnp.float32), stat(stats, 2), stat(stats, 3))
    out_ref[...] = p_ref[...].astype(jnp.float32) + STEP_SIZE * (cross - own)
    slots(rows, 0, chips - 1, row_send, row_recv.at[0]).wait_send()
    slots(cols, 0, n_grp - 1, col_send, col_recv).wait_send()
    forward_rows.wait_send()
    forward_cols.wait_send()
    swap.wait_send()
    got_s.wait_send()
    got_c.wait_send()


def per_device(n_ref, n_grp, particles, samples):
    part, d = particles.shape
    refs = samples.shape[0]
    chips, chunks = n_ref // 2, refs // CHUNK
    n_rows, half = n_ref * part, n_ref * part // 2
    dma = pltpu.SemaphoreType.DMA
    bf16, f32 = jnp.bfloat16, jnp.float32
    return pl.pallas_call(
        kernel,
        out_shape=jax.ShapeDtypeStruct((part, d), f32),
        in_specs=[pl.BlockSpec(memory_space=pl.ANY)] * 2,
        out_specs=pl.BlockSpec(memory_space=pltpu.VMEM),
        scratch_shapes=[
            pltpu.VMEM((part, d), bf16),
            pltpu.VMEM((chunks, CHUNK, d), bf16),
            pltpu.VMEM((n_ref, part, d), bf16),
            pltpu.VMEM((2 * n_grp, part, d), bf16),
            pltpu.VMEM((n_rows, d), bf16),
            pltpu.VMEM((chunks, 1, CHUNK), f32),
            pltpu.VMEM((chunks, n_rows, CHUNK), f32),
            pltpu.VMEM((n_rows, d), f32),
            pltpu.VMEM((half, d + LANES), bf16),
            pltpu.VMEM((half, d + LANES), bf16),
            pltpu.VMEM((chips, part, d + LANES), bf16),
            pltpu.VMEM((chips, part, d + LANES), bf16),
            pltpu.VMEM((chips, part, d), bf16),
            pltpu.VMEM((chips, part, d), bf16),
            dma((chunks,)), dma, dma, dma((Z,)), dma, dma, dma, dma, dma, dma,
            dma, dma, dma, dma, dma, dma,
        ],
        compiler_params=pltpu.CompilerParams(
            collective_id=0, has_side_effects=True, vmem_limit_bytes=VMEM_BYTES
        ),
        name="mmd_step",
    )(particles, samples)


def solution(mesh):
    step = functools.partial(per_device, mesh.shape["ref"], mesh.shape["grp"])
    return jax.shard_map(
        step,
        mesh=mesh,
        in_specs=(P(("grp", "ref"), None), P("ref", None)),
        out_specs=P(("grp", "ref"), None),
        check_vma=False,
    )
```

```python
import functools
import math

import jax
import jax.numpy as jnp
from jax import lax
from jax.experimental import pallas as pl
from jax.experimental.pallas import tpu as pltpu
from jax.sharding import PartitionSpec as P

KERNEL_WIDTH = 16
STEP_SIZE = 8.0
MASKED = -1e30
SCALE = math.log2(math.e) / (2.0 * KERNEL_WIDTH)
MESH = pl.DeviceIdType.MESH
CHUNK = 512
LATE = 3
LANES = 128
VMEM_BYTES = 56 * 2**20
Z, Y, LO = 4, 4, 2


def packed(part, *columns):
    rows, n = columns[0].shape[0], len(columns)
    lane = lax.broadcasted_iota(jnp.int32, (rows, LANES), 1)
    row = lax.broadcasted_iota(jnp.int32, (rows, LANES), 0) % part
    line = jnp.zeros((rows, LANES), jnp.float32)
    for k, column in enumerate(columns):
        line = jnp.where(lane == row * n + k, column, line)
    return jnp.sum(line.reshape(rows // part, part, LANES), axis=1, keepdims=True)


def unpacked(lines, part, n):
    shape = (lines.shape[0], part, LANES)
    lane = lax.broadcasted_iota(jnp.int32, shape, 2)
    row = lax.broadcasted_iota(jnp.int32, shape, 1)
    wide = jnp.broadcast_to(lines, shape)
    return [
        jnp.sum(jnp.where(lane == row * n + k, wide, 0.0), axis=2, keepdims=True) for k in range(n)
    ]


def merged_mean(parts, top, mass):
    share = jnp.exp2(top - jnp.max(top, axis=0, keepdims=True))
    return jnp.sum(share * parts, axis=0) / jnp.sum(share * mass, axis=0)


def turned(values):
    across = values.T
    wide = across.astype(jnp.float32)
    return across, jnp.sum(wide * wide, axis=0, keepdims=True)


def dot(a, b):
    return jnp.dot(a, b, preferred_element_type=jnp.float32)


def kernel(
    p_hbm, samples_ref, out_ref,
    p_ref, smp, turn, rows, cols, pmat, ref_sq, scores, acc,
    send_c, recv_c, send_s, recv_s, send_t, recv_t,
    load_sem, p_sem, row_send, row_recv, col_send, col_recv, smp_send, smp_recv,
    c_send, c_recv, s_send, s_recv, t_send, t_recv,
):
    n_grp = lax.axis_size("grp")
    me, mine = lax.axis_index("ref"), lax.axis_index("grp")
    core, y, zh = me % 2, (me // 2) % Y, me // (2 * Y)
    mate = me + 1 - 2 * core
    part, d = p_ref.shape
    chips = Z * Y
    half = chips * part
    chunks = smp.shape[0] // 2
    far_first = [(a, b) for a in (2, 1, 3, 0) for b in (2, 1, 3, 0) if (a, b) != (0, 0)]

    lo, x = mine % LO, mine // LO

    def goes_to(a, b):
        to_lo = (lo, 0, 1 - lo, 1)[a]
        where = {"grp": x * LO + to_lo, "ref": (((zh + a) % Z) * Y + (y + b) % Y) * 2 + core}
        return where, (0, 1 + 2 * lo, 2, 1 + 2 * lo)[a] * Y + b

    def z_of_slot(s):
        if s == 0:
            return zh, lo
        if s == 2:
            return (zh + 2) % Z, 1 - lo
        return (zh + Z - 1 + 2 * lo) % Z, s // 2

    def comes_from(s, b):
        from_zh, from_lo = z_of_slot(s)
        return {"grp": x * LO + from_lo, "ref": (from_zh * Y + (y + Y - b) % Y) * 2 + core}

    def returns_to(s, b):
        return comes_from(s, b), (0, 1 + 2 * lo, 2, 1 + 2 * lo)[s] * Y + b

    def remote(src, dst, send_sem, recv_sem, **where):
        return pltpu.make_async_remote_copy(
            src, dst, send_sem, recv_sem, device_id=where, device_id_type=MESH
        )

    barrier = pltpu.get_barrier_semaphore()
    for a, b in far_first:
        pl.semaphore_signal(barrier, inc=1, device_id=comes_from(a, b), device_id_type=MESH)
    for j in range(1, n_grp):
        pl.semaphore_signal(barrier, inc=1, device_id={"grp": (mine + j) % n_grp}, device_id_type=MESH)
    for j in range(n_grp):
        where = {"grp": (mine + j) % n_grp, "ref": mate}
        pl.semaphore_signal(barrier, inc=1, device_id=where, device_id_type=MESH)

    load_p = pltpu.make_async_copy(p_hbm, p_ref, p_sem)
    load_p.start()

    def load(j):
        return pltpu.make_async_copy(
            samples_ref.at[pl.ds(j * CHUNK, CHUNK)], smp.at[j], load_sem.at[j]
        )

    for j in range(chunks):
        load(j).start()

    load_p.wait()
    rows[0] = p_ref[...]
    cols[0] = p_ref[...]

    def take(j):
        across, square = turned(smp[j])
        turn[j] = across
        ref_sq[j] = square * SCALE

    def take_own(j, c):
        load(j).wait()
        take(j)
        return c

    pl.semaphore_wait(barrier, chips - 1 + n_grp - 1 + n_grp)

    for a, b in far_first:
        where, slot = goes_to(a, b)
        remote(p_ref, rows.at[slot], row_send, row_recv, **where).start()

    for j in range(1, n_grp):
        remote(p_ref, cols.at[j], col_send, col_recv, grp=(mine + j) % n_grp).start()
    for j in range(n_grp):
        where = {"grp": (mine + j) % n_grp, "ref": mate}
        remote(p_ref, cols.at[n_grp + j], col_send, col_recv, **where).start()

    def pass_on(j):
        return remote(smp.at[j], smp.at[chunks + j], smp_send, smp_recv.at[j], ref=mate)

    def take_other(j, c):
        pass_on(j).wait_recv()
        take(chunks + j)
        return c


    def pass_first(j, c):
        load(j).wait()
        pass_on(j).start()
        return c

    for j in range(0):
        pass_on(j).start()
    lax.fori_loop(0, chunks, pass_first, 0)

    def take_rest(j, c):
        take(j)
        return c

    lax.fori_loop(0, chunks, take_rest, 0)
    lax.fori_loop(0, chunks - LATE, take_other, 0)

    def slots(buf, start, n, send_sem, recv_sem):
        return remote(buf.at[pl.ds(start, n)], buf.at[pl.ds(start, n)], send_sem, recv_sem, ref=mate)

    got_rows = slots(rows, 0, chips - 1, row_send, row_recv)
    got_rows.wait_recv()
    wide = rows[...].astype(jnp.float32).reshape(half, d)
    pmat[...] = wide.astype(jnp.bfloat16)
    row_sq = jnp.sum(wide * wide, axis=1, keepdims=True)
    n = Y * part
    center = jnp.sum(wide.reshape(Z, n, d), axis=1, keepdims=True) * (1.0 / n)
    of_mean = jnp.sum(center * center, axis=2, keepdims=True)
    of_rows = jnp.sum(row_sq.reshape(Z, n, 1), axis=1, keepdims=True) * (1.0 / n)
    noise = (of_rows - of_mean) * (1.0 / (n - 1))
    center = center * jnp.maximum(1.0 - noise / jnp.maximum(of_mean, 1e-30), 0.0)
    row_sq = row_sq * SCALE

    def less_center(total, mass):
        parted = total.reshape(Z, Y * part, d) - mass.reshape(Z, Y * part, 1) * center
        return parted.reshape(half, d)

    got_cols = slots(cols, 0, 2 * n_grp - 1, col_send, col_recv)
    got_cols.wait_recv()
    cmat = cols[...].astype(jnp.float32).reshape(2 * n_grp * part, d).astype(jnp.bfloat16)
    cturn, col_sq = turned(cmat)
    n_cols = 2 * n_grp * part

    s = (dot(pmat[...], cturn) * 2.0 - col_sq) * SCALE
    r = lax.broadcasted_iota(jnp.int32, (half, 1), 0)
    a, b = r // (Y * part), (r // part) % Y
    row_base = jnp.zeros((half, 1), jnp.int32)
    for n in range(Z):
        from_zh, from_lo = z_of_slot(n)
        base = (x * LO + from_lo) * (2 * half) + (from_zh * Y * 2 + core) * part
        row_base = jnp.where(a == n, base, row_base)
    row_id = row_base + ((y + Y - b) % Y) * (2 * part) + r % part
    q = lax.broadcasted_iota(jnp.int32, (1, n_cols), 1)
    j = (q // part) % n_grp
    col_id = (
        (mine + n_grp - j) % n_grp * (2 * half)
        + jnp.where(q < n_grp * part, me, mate) * part
        + q % part
    )
    same = row_id == col_id
    s = jnp.where(same, MASKED, s)
    s_top = jnp.max(s, axis=1, keepdims=True)
    w = jnp.where(same, 0.0, jnp.exp2(s - s_top))
    s_mass = jnp.sum(w, axis=1, keepdims=True)
    s_sum = dot(w.astype(jnp.bfloat16), cmat)
    send_s[...] = less_center(s_sum, s_mass).reshape(chips, part, d).astype(jnp.bfloat16)

    for a, b in far_first:
        where, slot = returns_to(a, b)
        remote(send_s.at[a * Y + b], recv_s.at[slot], s_send, s_recv, **where).start()
    recv_s[0] = send_s[0]

    top = jnp.full((half, LANES), -jnp.inf, jnp.float32)
    for j in range(2 * chunks):
        if j >= 2 * chunks - LATE:
            pass_on(j - chunks).wait_recv()
            take(j)
        s = dot(pmat[...], turn[j]) * (2.0 * SCALE) - ref_sq[j]
        scores[j] = s
        for at in range(0, CHUNK, LANES):
            top = jnp.maximum(top, s[:, at : at + LANES])
    top = jnp.max(top, axis=1, keepdims=True)
    mass = jnp.zeros((half, LANES), jnp.float32)
    for j in range(2 * chunks):
        w = jnp.exp2(scores[j] - top)
        for at in range(0, CHUNK, LANES):
            mass = mass + w[:, at : at + LANES]
        term = dot(w.astype(jnp.bfloat16), smp[j])
        if j == 0:
            acc[...] = term
        else:
            acc[...] += term
    mass = jnp.sum(mass, axis=1, keepdims=True)
    send_t[...] = packed(part, top - row_sq, mass, s_top - row_sq, s_mass)
    for a, b in far_first:
        where, slot = returns_to(a, b)
        remote(send_t.at[a * Y + b], recv_t.at[slot], t_send, t_recv, **where).start()
    recv_t[0] = send_t[0]
    total = less_center(acc[...], mass)
    send_c[...] = total.reshape(chips, part, d).astype(jnp.bfloat16)

    for a, b in far_first:
        where, slot = returns_to(a, b)
        remote(send_c.at[a * Y + b], recv_c.at[slot], c_send, c_recv, **where).start()
    recv_c[0] = send_c[0]

    got_s = slots(recv_s, 0, chips - 1, s_send, s_recv)
    got_c = slots(recv_c, 0, chips - 1, c_send, c_recv)
    got_t = slots(recv_t, 0, chips - 1, t_send, t_recv)
    got_s.wait_recv()
    got_t.wait_recv()
    c_top, c_mass, s_top, s_mass = unpacked(recv_t[...], part, 4)
    own = merged_mean(recv_s[...].astype(jnp.float32), s_top, s_mass)
    got_c.wait_recv()
    cross = merged_mean(recv_c[...].astype(jnp.float32), c_top, c_mass)
    out_ref[...] = p_ref[...].astype(jnp.float32) + STEP_SIZE * (cross - own)
    got_rows.wait_send()
    got_cols.wait_send()
    slots(smp, 0, chunks, smp_send, smp_recv.at[0]).wait_send()
    got_s.wait_send()
    got_c.wait_send()
    got_t.wait_send()


def per_device(n_ref, n_grp, particles, samples):
    part, d = particles.shape
    refs = samples.shape[0]
    chips, chunks = n_ref // 2, refs // CHUNK
    half = chips * part
    dma = pltpu.SemaphoreType.DMA
    bf16, f32 = jnp.bfloat16, jnp.float32
    return pl.pallas_call(
        kernel,
        out_shape=pltpu.VMEM((part, d), f32),
        in_specs=[pl.BlockSpec(memory_space=pl.ANY)] * 2,
        out_specs=pl.BlockSpec(memory_space=pltpu.VMEM),
        scratch_shapes=[
            pltpu.VMEM((part, d), bf16),
            pltpu.VMEM((2 * chunks, CHUNK, d), bf16),
            pltpu.VMEM((2 * chunks, d, CHUNK), bf16),
            pltpu.VMEM((chips, part, d), bf16),
            pltpu.VMEM((2 * n_grp, part, d), bf16),
            pltpu.VMEM((half, d), bf16),
            pltpu.VMEM((2 * chunks, 1, CHUNK), f32),
            pltpu.VMEM((2 * chunks, half, CHUNK), f32),
            pltpu.VMEM((half, d), f32),
            pltpu.VMEM((chips, part, d), bf16),
            pltpu.VMEM((chips, part, d), bf16),
            pltpu.VMEM((chips, part, d), bf16),
            pltpu.VMEM((chips, part, d), bf16),
            pltpu.VMEM((chips, 1, LANES), f32),
            pltpu.VMEM((chips, 1, LANES), f32),
            dma((chunks,)), dma, dma, dma, dma, dma, dma, dma((chunks,)),
            dma, dma, dma, dma, dma, dma,
        ],
        compiler_params=pltpu.CompilerParams(
            collective_id=0, has_side_effects=True, vmem_limit_bytes=VMEM_BYTES
        ),
        name="mmd_step",
    )(particles, samples)


def solution(mesh):
    step = functools.partial(per_device, mesh.shape["ref"], mesh.shape["grp"])
    return jax.shard_map(
        step,
        mesh=mesh,
        in_specs=(P(("grp", "ref"), None), P("ref", None)),
        out_specs=P(("grp", "ref"), None),
        check_vma=False,
    )
```

```python
import functools
import math

import jax
import jax.numpy as jnp
from jax import lax
from jax.experimental import pallas as pl
from jax.experimental.pallas import tpu as pltpu
from jax.sharding import PartitionSpec as P

KERNEL_WIDTH = 16
STEP_SIZE = 8.0
MASKED = -1e30
SCALE = math.log2(math.e) / (2.0 * KERNEL_WIDTH)
MESH = pl.DeviceIdType.MESH
CHUNK = 512
LATE = 3
LANES = 128
VMEM_BYTES = 56 * 2**20
Z, Y, LO = 4, 4, 2


def packed(part, *columns):
    rows, n = columns[0].shape[0], len(columns)
    lane = lax.broadcasted_iota(jnp.int32, (rows, LANES), 1)
    row = lax.broadcasted_iota(jnp.int32, (rows, LANES), 0) % part
    line = jnp.zeros((rows, LANES), jnp.float32)
    for k, column in enumerate(columns):
        line = jnp.where(lane == row * n + k, column, line)
    return jnp.sum(line.reshape(rows // part, part, LANES), axis=1, keepdims=True)


def unpacked(lines, part, n):
    shape = (lines.shape[0], part, LANES)
    lane = lax.broadcasted_iota(jnp.int32, shape, 2)
    row = lax.broadcasted_iota(jnp.int32, shape, 1)
    wide = jnp.broadcast_to(lines, shape)
    return [
        jnp.sum(jnp.where(lane == row * n + k, wide, 0.0), axis=2, keepdims=True) for k in range(n)
    ]


def shares(top, mass):
    share = jnp.exp2(top - jnp.max(top, axis=0, keepdims=True))
    return share / jnp.sum(share * mass, axis=0, keepdims=True)


def turned(values):
    across = values.T
    wide = across.astype(jnp.float32)
    return across, jnp.sum(wide * wide, axis=0, keepdims=True)


def dot(a, b):
    return jnp.dot(a, b, preferred_element_type=jnp.float32)


def kernel(
    p_hbm, samples_ref, out_ref,
    p_ref, smp, turn, rows, cols, pmat, ref_sq, scores, acc,
    send_c, recv_c, send_s, recv_s, send_t, recv_t,
    load_sem, p_sem, row_send, row_recv, col_send, col_recv, smp_send, smp_recv,
    c_send, c_recv, s_send, s_recv, t_send, t_recv,
):
    n_grp = lax.axis_size("grp")
    me, mine = lax.axis_index("ref"), lax.axis_index("grp")
    core, y, zh = me % 2, (me // 2) % Y, me // (2 * Y)
    mate = me + 1 - 2 * core
    part, d = p_ref.shape
    chips = Z * Y
    half = chips * part
    chunks = smp.shape[0] // 2
    far_first = [(a, b) for a in (2, 1, 3, 0) for b in (2, 1, 3, 0) if (a, b) != (0, 0)]

    lo, x = mine % LO, mine // LO

    def goes_to(a, b):
        to_lo = (lo, 0, 1 - lo, 1)[a]
        where = {"grp": x * LO + to_lo, "ref": (((zh + a) % Z) * Y + (y + b) % Y) * 2 + core}
        return where, (0, 1 + 2 * lo, 2, 1 + 2 * lo)[a] * Y + b

    def z_of_slot(s):
        if s == 0:
            return zh, lo
        if s == 2:
            return (zh + 2) % Z, 1 - lo
        return (zh + Z - 1 + 2 * lo) % Z, s // 2

    def comes_from(s, b):
        from_zh, from_lo = z_of_slot(s)
        return {"grp": x * LO + from_lo, "ref": (from_zh * Y + (y + Y - b) % Y) * 2 + core}

    def returns_to(s, b):
        return comes_from(s, b), (0, 1 + 2 * lo, 2, 1 + 2 * lo)[s] * Y + b

    def remote(src, dst, send_sem, recv_sem, **where):
        return pltpu.make_async_remote_copy(
            src, dst, send_sem, recv_sem, device_id=where, device_id_type=MESH
        )

    barrier = pltpu.get_barrier_semaphore()
    for a, b in far_first:
        pl.semaphore_signal(barrier, inc=1, device_id=comes_from(a, b), device_id_type=MESH)
    for j in range(1, n_grp):
        pl.semaphore_signal(barrier, inc=1, device_id={"grp": (mine + j) % n_grp}, device_id_type=MESH)
    for j in range(n_grp):
        where = {"grp": (mine + j) % n_grp, "ref": mate}
        pl.semaphore_signal(barrier, inc=1, device_id=where, device_id_type=MESH)

    load_p = pltpu.make_async_copy(p_hbm, p_ref, p_sem)
    load_p.start()

    def load(j):
        return pltpu.make_async_copy(
            samples_ref.at[pl.ds(j * CHUNK, CHUNK)], smp.at[j], load_sem.at[j]
        )

    for j in range(chunks):
        load(j).start()

    load_p.wait()
    rows[0] = p_ref[...]
    cols[0] = p_ref[...]

    def take(j):
        across, square = turned(smp[j])
        turn[j] = across
        ref_sq[j] = square * SCALE

    def take_own(j, c):
        load(j).wait()
        take(j)
        return c

    pl.semaphore_wait(barrier, chips - 1 + n_grp - 1 + n_grp)

    for a, b in far_first:
        where, slot = goes_to(a, b)
        remote(p_ref, rows.at[slot], row_send, row_recv, **where).start()

    for j in range(1, n_grp):
        remote(p_ref, cols.at[j], col_send, col_recv, grp=(mine + j) % n_grp).start()
    for j in range(n_grp):
        where = {"grp": (mine + j) % n_grp, "ref": mate}
        remote(p_ref, cols.at[n_grp + j], col_send, col_recv, **where).start()

    def pass_on(j):
        return remote(smp.at[j], smp.at[chunks + j], smp_send, smp_recv.at[j], ref=mate)

    def take_other(j, c):
        pass_on(j).wait_recv()
        take(chunks + j)
        return c


    def pass_first(j, c):
        load(j).wait()
        pass_on(j).start()
        return c

    for j in range(0):
        pass_on(j).start()
    lax.fori_loop(0, chunks, pass_first, 0)

    def take_rest(j, c):
        take(j)
        return c

    lax.fori_loop(0, chunks, take_rest, 0)
    lax.fori_loop(0, chunks - LATE, take_other, 0)

    def slots(buf, start, n, send_sem, recv_sem):
        return remote(buf.at[pl.ds(start, n)], buf.at[pl.ds(start, n)], send_sem, recv_sem, ref=mate)

    got_rows = slots(rows, 0, chips - 1, row_send, row_recv)
    got_rows.wait_recv()
    wide = rows[...].astype(jnp.float32).reshape(half, d)
    pmat[...] = wide.astype(jnp.bfloat16)
    row_sq = jnp.sum(wide * wide, axis=1, keepdims=True)
    n = Y * part
    center = jnp.sum(wide.reshape(Z, n, d), axis=1, keepdims=True) * (1.0 / n)
    of_mean = jnp.sum(center * center, axis=2, keepdims=True)
    of_rows = jnp.sum(row_sq.reshape(Z, n, 1), axis=1, keepdims=True) * (1.0 / n)
    noise = (of_rows - of_mean) * (1.0 / (n - 1))
    center = center * jnp.maximum(1.0 - noise / jnp.maximum(of_mean, 1e-30), 0.0)
    row_sq = row_sq * SCALE

    def less_center(total, mass):
        parted = total.reshape(Z, Y * part, d) - mass.reshape(Z, Y * part, 1) * center
        return parted.reshape(half, d)

    got_cols = slots(cols, 0, 2 * n_grp - 1, col_send, col_recv)
    got_cols.wait_recv()
    cmat = cols[...].astype(jnp.float32).reshape(2 * n_grp * part, d).astype(jnp.bfloat16)
    cturn, col_sq = turned(cmat)
    n_cols = 2 * n_grp * part

    s = (dot(pmat[...], cturn) * 2.0 - col_sq) * SCALE
    r = lax.broadcasted_iota(jnp.int32, (half, 1), 0)
    a, b = r // (Y * part), (r // part) % Y
    row_base = jnp.zeros((half, 1), jnp.int32)
    for n in range(Z):
        from_zh, from_lo = z_of_slot(n)
        base = (x * LO + from_lo) * (2 * half) + (from_zh * Y * 2 + core) * part
        row_base = jnp.where(a == n, base, row_base)
    row_id = row_base + ((y + Y - b) % Y) * (2 * part) + r % part
    q = lax.broadcasted_iota(jnp.int32, (1, n_cols), 1)
    j = (q // part) % n_grp
    col_id = (
        (mine + n_grp - j) % n_grp * (2 * half)
        + jnp.where(q < n_grp * part, me, mate) * part
        + q % part
    )
    same = row_id == col_id
    s = jnp.where(same, MASKED, s)
    s_top = jnp.max(s, axis=1, keepdims=True)
    w = jnp.where(same, 0.0, jnp.exp2(s - s_top))
    s_mass = jnp.sum(w, axis=1, keepdims=True)
    s_sum = dot(w.astype(jnp.bfloat16), cmat)
    send_s[...] = less_center(s_sum, s_mass).reshape(chips, part, d).astype(jnp.bfloat16)


    top = jnp.full((half, LANES), -jnp.inf, jnp.float32)
    for j in range(2 * chunks):
        if j == 2 * chunks - LATE:
            for a, b in far_first:
                where, slot = returns_to(a, b)
                remote(send_s.at[a * Y + b], recv_s.at[slot], s_send, s_recv, **where).start()
            recv_s[0] = send_s[0]
        if j >= 2 * chunks - LATE:
            pass_on(j - chunks).wait_recv()
            take(j)
        s = dot(pmat[...], turn[j]) * (2.0 * SCALE) - ref_sq[j]
        scores[j] = s
        for at in range(0, CHUNK, LANES):
            top = jnp.maximum(top, s[:, at : at + LANES])
    top = jnp.max(top, axis=1, keepdims=True)
    mass = jnp.zeros((half, LANES), jnp.float32)
    for j in range(2 * chunks):
        w = jnp.exp2(scores[j] - top)
        for at in range(0, CHUNK, LANES):
            mass = mass + w[:, at : at + LANES]
        term = dot(w.astype(jnp.bfloat16), smp[j])
        if j == 0:
            acc[...] = term
        else:
            acc[...] += term
    mass = jnp.sum(mass, axis=1, keepdims=True)
    send_t[...] = packed(part, top - row_sq, mass, s_top - row_sq, s_mass)
    for a, b in far_first:
        where, slot = returns_to(a, b)
        remote(send_t.at[a * Y + b], recv_t.at[slot], t_send, t_recv, **where).start()
    recv_t[0] = send_t[0]
    total = less_center(acc[...], mass)
    send_c[...] = total.reshape(chips, part, d).astype(jnp.bfloat16)

    for a, b in far_first:
        where, slot = returns_to(a, b)
        remote(send_c.at[a * Y + b], recv_c.at[slot], c_send, c_recv, **where).start()
    recv_c[0] = send_c[0]

    got_s = slots(recv_s, 0, chips - 1, s_send, s_recv)
    got_c = slots(recv_c, 0, chips - 1, c_send, c_recv)
    got_t = slots(recv_t, 0, chips - 1, t_send, t_recv)
    got_s.wait_recv()
    got_t.wait_recv()
    c_top, c_mass, s_top, s_mass = unpacked(recv_t[...], part, 4)
    wide = p_ref[...].astype(jnp.float32)
    s_share = shares(s_top, s_mass) * STEP_SIZE
    c_share = jnp.broadcast_to(shares(c_top, c_mass) * STEP_SIZE, (chips, part, LANES))
    out_ref[...] = wide - jnp.sum(s_share * recv_s[...].astype(jnp.float32), axis=0)
    got_c.wait_recv()
    for at in range(0, d, LANES):
        lanes = pl.ds(at, LANES)
        out_ref[:, lanes] += jnp.sum(c_share * recv_c[:, :, lanes].astype(jnp.float32), axis=0)
    got_rows.wait_send()
    got_cols.wait_send()
    slots(smp, 0, chunks, smp_send, smp_recv.at[0]).wait_send()
    got_s.wait_send()
    got_c.wait_send()
    got_t.wait_send()


def per_device(n_ref, n_grp, particles, samples):
    part, d = particles.shape
    refs = samples.shape[0]
    chips, chunks = n_ref // 2, refs // CHUNK
    half = chips * part
    dma = pltpu.SemaphoreType.DMA
    bf16, f32 = jnp.bfloat16, jnp.float32
    return pl.pallas_call(
        kernel,
        out_shape=pltpu.VMEM((part, d), f32),
        in_specs=[pl.BlockSpec(memory_space=pl.ANY)] * 2,
        out_specs=pl.BlockSpec(memory_space=pltpu.VMEM),
        scratch_shapes=[
            pltpu.VMEM((part, d), bf16),
            pltpu.VMEM((2 * chunks, CHUNK, d), bf16),
            pltpu.VMEM((2 * chunks, d, CHUNK), bf16),
            pltpu.VMEM((chips, part, d), bf16),
            pltpu.VMEM((2 * n_grp, part, d), bf16),
            pltpu.VMEM((half, d), bf16),
            pltpu.VMEM((2 * chunks, 1, CHUNK), f32),
            pltpu.VMEM((2 * chunks, half, CHUNK), f32),
            pltpu.VMEM((half, d), f32),
            pltpu.VMEM((chips, part, d), bf16),
            pltpu.VMEM((chips, part, d), bf16),
            pltpu.VMEM((chips, part, d), bf16),
            pltpu.VMEM((chips, part, d), bf16),
            pltpu.VMEM((chips, 1, LANES), f32),
            pltpu.VMEM((chips, 1, LANES), f32),
            dma((chunks,)), dma, dma, dma, dma, dma, dma, dma((chunks,)),
            dma, dma, dma, dma, dma, dma,
        ],
        compiler_params=pltpu.CompilerParams(
            collective_id=0, has_side_effects=True, vmem_limit_bytes=VMEM_BYTES
        ),
        name="mmd_step",
    )(particles, samples)


def solution(mesh):
    step = functools.partial(per_device, mesh.shape["ref"], mesh.shape["grp"])
    return jax.shard_map(
        step,
        mesh=mesh,
        in_specs=(P(("grp", "ref"), None), P("ref", None)),
        out_specs=P(("grp", "ref"), None),
        check_vma=False,
    )
```

```python
import functools
import math

import jax
import jax.numpy as jnp
from jax import lax
from jax.experimental import pallas as pl
from jax.experimental.pallas import tpu as pltpu
from jax.sharding import PartitionSpec as P

KERNEL_WIDTH = 16
STEP_SIZE = 8.0
MASKED = -1e30
SCALE = math.log2(math.e) / (2.0 * KERNEL_WIDTH)
MESH = pl.DeviceIdType.MESH
CHUNK = 1024
LATE = 1
LANES = 128
VMEM_BYTES = 56 * 2**20
Z, Y, LO = 4, 4, 2


def packed(part, *columns):
    rows, n = columns[0].shape[0], len(columns)
    lane = lax.broadcasted_iota(jnp.int32, (rows, LANES), 1)
    row = lax.broadcasted_iota(jnp.int32, (rows, LANES), 0) % part
    line = jnp.zeros((rows, LANES), jnp.float32)
    for k, column in enumerate(columns):
        line = jnp.where(lane == row * n + k, column, line)
    return jnp.sum(line.reshape(rows // part, part, LANES), axis=1, keepdims=True)


def unpacked(lines, part, n):
    shape = (lines.shape[0], part, LANES)
    lane = lax.broadcasted_iota(jnp.int32, shape, 2)
    row = lax.broadcasted_iota(jnp.int32, shape, 1)
    wide = jnp.broadcast_to(lines, shape)
    return [
        jnp.sum(jnp.where(lane == row * n + k, wide, 0.0), axis=2, keepdims=True) for k in range(n)
    ]


def shares(top, mass):
    share = jnp.exp2(top - jnp.max(top, axis=0, keepdims=True))
    return share / jnp.sum(share * mass, axis=0, keepdims=True)


def turned(values):
    across = values.T
    wide = across.astype(jnp.float32)
    return across, jnp.sum(wide * wide, axis=0, keepdims=True)


def dot(a, b):
    return jnp.dot(a, b, preferred_element_type=jnp.float32)


def kernel(
    p_hbm, samples_ref, out_ref,
    p_ref, smp, turn, rows, cols, pmat, ref_sq, scores, acc,
    send_c, recv_c, send_s, recv_s, send_t, recv_t,
    load_sem, p_sem, row_send, row_recv, col_send, col_recv, smp_send, smp_recv,
    c_send, c_recv, s_send, s_recv, t_send, t_recv,
):
    n_grp = lax.axis_size("grp")
    me, mine = lax.axis_index("ref"), lax.axis_index("grp")
    core, y, zh = me % 2, (me // 2) % Y, me // (2 * Y)
    mate = me + 1 - 2 * core
    part, d = p_ref.shape
    chips = Z * Y
    half = chips * part
    chunks = smp.shape[0] // 2
    far_first = [(a, b) for a in (2, 1, 3, 0) for b in (2, 1, 3, 0) if (a, b) != (0, 0)]

    lo, x = mine % LO, mine // LO

    def goes_to(a, b):
        to_lo = (lo, 0, 1 - lo, 1)[a]
        where = {"grp": x * LO + to_lo, "ref": (((zh + a) % Z) * Y + (y + b) % Y) * 2 + core}
        return where, (0, 1 + 2 * lo, 2, 1 + 2 * lo)[a] * Y + b

    def z_of_slot(s):
        if s == 0:
            return zh, lo
        if s == 2:
            return (zh + 2) % Z, 1 - lo
        return (zh + Z - 1 + 2 * lo) % Z, s // 2

    def comes_from(s, b):
        from_zh, from_lo = z_of_slot(s)
        return {"grp": x * LO + from_lo, "ref": (from_zh * Y + (y + Y - b) % Y) * 2 + core}

    def returns_to(s, b):
        return comes_from(s, b), (0, 1 + 2 * lo, 2, 1 + 2 * lo)[s] * Y + b

    def remote(src, dst, send_sem, recv_sem, **where):
        return pltpu.make_async_remote_copy(
            src, dst, send_sem, recv_sem, device_id=where, device_id_type=MESH
        )

    barrier = pltpu.get_barrier_semaphore()
    for a, b in far_first:
        pl.semaphore_signal(barrier, inc=1, device_id=comes_from(a, b), device_id_type=MESH)
    for j in range(1, n_grp):
        pl.semaphore_signal(barrier, inc=1, device_id={"grp": (mine + j) % n_grp}, device_id_type=MESH)
    for j in range(n_grp):
        where = {"grp": (mine + j) % n_grp, "ref": mate}
        pl.semaphore_signal(barrier, inc=1, device_id=where, device_id_type=MESH)

    load_p = pltpu.make_async_copy(p_hbm, p_ref, p_sem)
    load_p.start()

    def load(j):
        return pltpu.make_async_copy(
            samples_ref.at[pl.ds(j * CHUNK, CHUNK)], smp.at[j], load_sem.at[j]
        )

    for j in range(chunks):
        load(j).start()

    load_p.wait()
    rows[0] = p_ref[...]
    cols[0] = p_ref[...]

    def take(j):
        across, square = turned(smp[j])
        turn[j] = across
        ref_sq[j] = square * SCALE

    def take_own(j, c):
        load(j).wait()
        take(j)
        return c

    pl.semaphore_wait(barrier, chips - 1 + n_grp - 1 + n_grp)

    for a, b in far_first:
        where, slot = goes_to(a, b)
        remote(p_ref, rows.at[slot], row_send, row_recv, **where).start()

    for j in range(1, n_grp):
        remote(p_ref, cols.at[j], col_send, col_recv, grp=(mine + j) % n_grp).start()
    for j in range(n_grp):
        where = {"grp": (mine + j) % n_grp, "ref": mate}
        remote(p_ref, cols.at[n_grp + j], col_send, col_recv, **where).start()

    def pass_on(j):
        return remote(smp.at[j], smp.at[chunks + j], smp_send, smp_recv.at[j], ref=mate)

    def take_other(j, c):
        pass_on(j).wait_recv()
        take(chunks + j)
        return c


    def pass_first(j, c):
        load(j).wait()
        pass_on(j).start()
        return c

    for j in range(0):
        pass_on(j).start()
    lax.fori_loop(0, chunks, pass_first, 0)

    def take_rest(j, c):
        take(j)
        return c

    lax.fori_loop(0, chunks, take_rest, 0)
    lax.fori_loop(0, chunks - LATE, take_other, 0)

    def slots(buf, start, n, send_sem, recv_sem):
        return remote(buf.at[pl.ds(start, n)], buf.at[pl.ds(start, n)], send_sem, recv_sem, ref=mate)

    got_rows = slots(rows, 0, chips - 1, row_send, row_recv)
    got_rows.wait_recv()
    wide = rows[...].astype(jnp.float32).reshape(half, d)
    pmat[...] = wide.astype(jnp.bfloat16)
    row_sq = jnp.sum(wide * wide, axis=1, keepdims=True)
    n = Y * part
    center = jnp.sum(wide.reshape(Z, n, d), axis=1, keepdims=True) * (1.0 / n)
    of_mean = jnp.sum(center * center, axis=2, keepdims=True)
    of_rows = jnp.sum(row_sq.reshape(Z, n, 1), axis=1, keepdims=True) * (1.0 / n)
    noise = (of_rows - of_mean) * (1.0 / (n - 1))
    center = center * jnp.maximum(1.0 - noise / jnp.maximum(of_mean, 1e-30), 0.0)
    row_sq = row_sq * SCALE

    def less_center(total, mass):
        parted = total.reshape(Z, Y * part, d) - mass.reshape(Z, Y * part, 1) * center
        return parted.reshape(half, d)

    got_cols = slots(cols, 0, 2 * n_grp - 1, col_send, col_recv)
    got_cols.wait_recv()
    cmat = cols[...].astype(jnp.float32).reshape(2 * n_grp * part, d).astype(jnp.bfloat16)
    cturn, col_sq = turned(cmat)
    n_cols = 2 * n_grp * part

    s = (dot(pmat[...], cturn) * 2.0 - col_sq) * SCALE
    r = lax.broadcasted_iota(jnp.int32, (half, 1), 0)
    a, b = r // (Y * part), (r // part) % Y
    row_base = jnp.zeros((half, 1), jnp.int32)
    for n in range(Z):
        from_zh, from_lo = z_of_slot(n)
        base = (x * LO + from_lo) * (2 * half) + (from_zh * Y * 2 + core) * part
        row_base = jnp.where(a == n, base, row_base)
    row_id = row_base + ((y + Y - b) % Y) * (2 * part) + r % part
    q = lax.broadcasted_iota(jnp.int32, (1, n_cols), 1)
    j = (q // part) % n_grp
    col_id = (
        (mine + n_grp - j) % n_grp * (2 * half)
        + jnp.where(q < n_grp * part, me, mate) * part
        + q % part
    )
    same = row_id == col_id
    s = jnp.where(same, MASKED, s)
    s_top = jnp.max(s, axis=1, keepdims=True)
    w = jnp.where(same, 0.0, jnp.exp2(s - s_top))
    s_mass = jnp.sum(w, axis=1, keepdims=True)
    s_sum = dot(w.astype(jnp.bfloat16), cmat)
    send_s[...] = less_center(s_sum, s_mass).reshape(chips, part, d).astype(jnp.bfloat16)


    top = jnp.full((half, LANES), -jnp.inf, jnp.float32)
    for j in range(2 * chunks):
        if j == 2 * chunks - LATE:
            for a, b in far_first:
                where, slot = returns_to(a, b)
                remote(send_s.at[a * Y + b], recv_s.at[slot], s_send, s_recv, **where).start()
            recv_s[0] = send_s[0]
        if j >= 2 * chunks - LATE:
            pass_on(j - chunks).wait_recv()
            take(j)
        s = dot(pmat[...], turn[j]) * (2.0 * SCALE) - ref_sq[j]
        scores[j] = s
        for at in range(0, CHUNK, LANES):
            top = jnp.maximum(top, s[:, at : at + LANES])
    top = jnp.max(top, axis=1, keepdims=True)
    mass = jnp.zeros((half, LANES), jnp.float32)
    for j in range(2 * chunks):
        w = jnp.exp2(scores[j] - top)
        for at in range(0, CHUNK, LANES):
            mass = mass + w[:, at : at + LANES]
        term = dot(w.astype(jnp.bfloat16), smp[j])
        if j == 0:
            acc[...] = term
        else:
            acc[...] += term
    mass = jnp.sum(mass, axis=1, keepdims=True)
    send_t[...] = packed(part, top - row_sq, mass, s_top - row_sq, s_mass)
    for a, b in far_first:
        where, slot = returns_to(a, b)
        remote(send_t.at[a * Y + b], recv_t.at[slot], t_send, t_recv, **where).start()
    recv_t[0] = send_t[0]
    total = less_center(acc[...], mass)
    send_c[...] = total.reshape(chips, part, d).astype(jnp.bfloat16)

    for a, b in far_first:
        where, slot = returns_to(a, b)
        remote(send_c.at[a * Y + b], recv_c.at[slot], c_send, c_recv, **where).start()
    recv_c[0] = send_c[0]

    got_s = slots(recv_s, 0, chips - 1, s_send, s_recv)
    got_c = slots(recv_c, 0, chips - 1, c_send, c_recv)
    got_t = slots(recv_t, 0, chips - 1, t_send, t_recv)
    got_s.wait_recv()
    got_t.wait_recv()
    c_top, c_mass, s_top, s_mass = unpacked(recv_t[...], part, 4)
    wide = p_ref[...].astype(jnp.float32)
    s_share = shares(s_top, s_mass) * STEP_SIZE
    c_share = jnp.broadcast_to(shares(c_top, c_mass) * STEP_SIZE, (chips, part, LANES))
    out_ref[...] = wide - jnp.sum(s_share * recv_s[...].astype(jnp.float32), axis=0)
    got_c.wait_recv()
    for at in range(0, d, LANES):
        lanes = pl.ds(at, LANES)
        out_ref[:, lanes] += jnp.sum(c_share * recv_c[:, :, lanes].astype(jnp.float32), axis=0)
    got_rows.wait_send()
    got_cols.wait_send()
    slots(smp, 0, chunks, smp_send, smp_recv.at[0]).wait_send()
    got_s.wait_send()
    got_c.wait_send()
    got_t.wait_send()


def per_device(n_ref, n_grp, particles, samples):
    part, d = particles.shape
    refs = samples.shape[0]
    chips, chunks = n_ref // 2, refs // CHUNK
    half = chips * part
    dma = pltpu.SemaphoreType.DMA
    bf16, f32 = jnp.bfloat16, jnp.float32
    return pl.pallas_call(
        kernel,
        out_shape=pltpu.VMEM((part, d), f32),
        in_specs=[pl.BlockSpec(memory_space=pl.ANY)] * 2,
        out_specs=pl.BlockSpec(memory_space=pltpu.VMEM),
        scratch_shapes=[
            pltpu.VMEM((part, d), bf16),
            pltpu.VMEM((2 * chunks, CHUNK, d), bf16),
            pltpu.VMEM((2 * chunks, d, CHUNK), bf16),
            pltpu.VMEM((chips, part, d), bf16),
            pltpu.VMEM((2 * n_grp, part, d), bf16),
            pltpu.VMEM((half, d), bf16),
            pltpu.VMEM((2 * chunks, 1, CHUNK), f32),
            pltpu.VMEM((2 * chunks, half, CHUNK), f32),
            pltpu.VMEM((half, d), f32),
            pltpu.VMEM((chips, part, d), bf16),
            pltpu.VMEM((chips, part, d), bf16),
            pltpu.VMEM((chips, part, d), bf16),
            pltpu.VMEM((chips, part, d), bf16),
            pltpu.VMEM((chips, 1, LANES), f32),
            pltpu.VMEM((chips, 1, LANES), f32),
            dma((chunks,)), dma, dma, dma, dma, dma, dma, dma((chunks,)),
            dma, dma, dma, dma, dma, dma,
        ],
        compiler_params=pltpu.CompilerParams(
            collective_id=0, has_side_effects=True, vmem_limit_bytes=VMEM_BYTES
        ),
        name="mmd_step",
    )(particles, samples)


def solution(mesh):
    step = functools.partial(per_device, mesh.shape["ref"], mesh.shape["grp"])
    return jax.shard_map(
        step,
        mesh=mesh,
        in_specs=(P(("grp", "ref"), None), P("ref", None)),
        out_specs=P(("grp", "ref"), None),
        check_vma=False,
    )
```

```python
import functools
import math

import jax
import jax.numpy as jnp
from jax import lax
from jax.experimental import pallas as pl
from jax.experimental.pallas import tpu as pltpu
from jax.sharding import PartitionSpec as P

KERNEL_WIDTH = 16
STEP_SIZE = 8.0
MASKED = -1e30
SCALE = math.log2(math.e) / (2.0 * KERNEL_WIDTH)
MESH = pl.DeviceIdType.MESH
CHUNK = 512
LATE = 3
LANES = 128
VMEM_BYTES = 56 * 2**20
Z, Y, LO = 4, 4, 2


def packed(part, *columns):
    rows, n = columns[0].shape[0], len(columns)
    lane = lax.broadcasted_iota(jnp.int32, (rows, LANES), 1)
    row = lax.broadcasted_iota(jnp.int32, (rows, LANES), 0) % part
    line = jnp.zeros((rows, LANES), jnp.float32)
    for k, column in enumerate(columns):
        line = jnp.where(lane == row * n + k, column, line)
    return jnp.sum(line.reshape(rows // part, part, LANES), axis=1, keepdims=True)


def unpacked(lines, part, n):
    shape = (lines.shape[0], part, LANES)
    lane = lax.broadcasted_iota(jnp.int32, shape, 2)
    row = lax.broadcasted_iota(jnp.int32, shape, 1)
    wide = jnp.broadcast_to(lines, shape)
    return [
        jnp.sum(jnp.where(lane == row * n + k, wide, 0.0), axis=2, keepdims=True) for k in range(n)
    ]


def shares(top, mass):
    share = jnp.exp2(top - jnp.max(top, axis=0, keepdims=True))
    return share / jnp.sum(share * mass, axis=0, keepdims=True)


def turned(values):
    across = values.T
    wide = across.astype(jnp.float32)
    return across, jnp.sum(wide * wide, axis=0, keepdims=True)


def dot(a, b):
    return jnp.dot(a, b, preferred_element_type=jnp.float32)


def kernel(
    p_hbm, samples_ref, out_ref,
    p_ref, smp, turn, rows, cols, pmat, ref_sq, scores, acc,
    send_c, recv_c, send_s, recv_s, send_t, recv_t,
    load_sem, p_sem, row_send, row_recv, col_send, col_recv, smp_send, smp_recv,
    c_send, c_recv, s_send, s_recv, t_send, t_recv,
):
    n_grp = lax.axis_size("grp")
    me, mine = lax.axis_index("ref"), lax.axis_index("grp")
    core, y, zh = me % 2, (me // 2) % Y, me // (2 * Y)
    mate = me + 1 - 2 * core
    part, d = p_ref.shape
    chips = Z * Y
    half = chips * part
    chunks = smp.shape[0] // 2
    far_first = [(a, b) for a in (2, 1, 3, 0) for b in (2, 1, 3, 0) if (a, b) != (0, 0)]

    lo, x = mine % LO, mine // LO

    def goes_to(a, b):
        to_lo = (lo, 0, 1 - lo, 1)[a]
        where = {"grp": x * LO + to_lo, "ref": (((zh + a) % Z) * Y + (y + b) % Y) * 2 + core}
        return where, (0, 1 + 2 * lo, 2, 1 + 2 * lo)[a] * Y + b

    def z_of_slot(s):
        if s == 0:
            return zh, lo
        if s == 2:
            return (zh + 2) % Z, 1 - lo
        return (zh + Z - 1 + 2 * lo) % Z, s // 2

    def comes_from(s, b):
        from_zh, from_lo = z_of_slot(s)
        return {"grp": x * LO + from_lo, "ref": (from_zh * Y + (y + Y - b) % Y) * 2 + core}

    def returns_to(s, b):
        return comes_from(s, b), (0, 1 + 2 * lo, 2, 1 + 2 * lo)[s] * Y + b

    def remote(src, dst, send_sem, recv_sem, **where):
        return pltpu.make_async_remote_copy(
            src, dst, send_sem, recv_sem, device_id=where, device_id_type=MESH
        )

    barrier = pltpu.get_barrier_semaphore()
    for a, b in far_first:
        pl.semaphore_signal(barrier, inc=1, device_id=comes_from(a, b), device_id_type=MESH)
    for j in range(1, n_grp):
        pl.semaphore_signal(barrier, inc=1, device_id={"grp": (mine + j) % n_grp}, device_id_type=MESH)
    for j in range(n_grp):
        where = {"grp": (mine + j) % n_grp, "ref": mate}
        pl.semaphore_signal(barrier, inc=1, device_id=where, device_id_type=MESH)

    load_p = pltpu.make_async_copy(p_hbm, p_ref, p_sem)
    load_p.start()

    def load(j):
        return pltpu.make_async_copy(
            samples_ref.at[pl.ds(j * CHUNK, CHUNK)], smp.at[j], load_sem.at[j]
        )

    for j in range(chunks):
        load(j).start()

    load_p.wait()
    rows[0] = p_ref[...]
    cols[0] = p_ref[...]

    def take(j):
        across, square = turned(smp[j])
        turn[j] = across
        ref_sq[j] = square * SCALE

    def take_own(j, c):
        load(j).wait()
        take(j)
        return c

    pl.semaphore_wait(barrier, chips - 1 + n_grp - 1 + n_grp)

    for a, b in far_first:
        where, slot = goes_to(a, b)
        remote(p_ref, rows.at[slot], row_send, row_recv, **where).start()

    for j in range(1, n_grp):
        remote(p_ref, cols.at[j], col_send, col_recv, grp=(mine + j) % n_grp).start()
    for j in range(n_grp):
        where = {"grp": (mine + j) % n_grp, "ref": mate}
        remote(p_ref, cols.at[n_grp + j], col_send, col_recv, **where).start()

    def pass_on(j):
        return remote(smp.at[j], smp.at[chunks + j], smp_send, smp_recv.at[j], ref=mate)

    def take_other(j, c):
        pass_on(j).wait_recv()
        take(chunks + j)
        return c


    def pass_first(j, c):
        load(j).wait()
        pass_on(j).start()
        return c

    for j in range(0):
        pass_on(j).start()
    lax.fori_loop(0, chunks, pass_first, 0)

    def take_rest(j, c):
        take(j)
        return c

    lax.fori_loop(0, chunks, take_rest, 0)
    lax.fori_loop(0, chunks - LATE, take_other, 0)

    def slots(buf, start, n, send_sem, recv_sem):
        return remote(buf.at[pl.ds(start, n)], buf.at[pl.ds(start, n)], send_sem, recv_sem, ref=mate)

    n_cols = 2 * n_grp * part
    r = lax.broadcasted_iota(jnp.int32, (half, 1), 0)
    a, b = r // (Y * part), (r // part) % Y
    row_base = jnp.zeros((half, 1), jnp.int32)
    for n in range(Z):
        from_zh, from_lo = z_of_slot(n)
        base = (x * LO + from_lo) * (2 * half) + (from_zh * Y * 2 + core) * part
        row_base = jnp.where(a == n, base, row_base)
    row_id = row_base + ((y + Y - b) % Y) * (2 * part) + r % part
    q = lax.broadcasted_iota(jnp.int32, (1, n_cols), 1)
    j = (q // part) % n_grp
    col_id = (
        (mine + n_grp - j) % n_grp * (2 * half)
        + jnp.where(q < n_grp * part, me, mate) * part
        + q % part
    )
    same = row_id == col_id

    got_rows = slots(rows, 0, chips - 1, row_send, row_recv)
    got_rows.wait_recv()
    wide = rows[...].astype(jnp.float32).reshape(half, d)
    pmat[...] = wide.astype(jnp.bfloat16)
    row_sq = jnp.sum(wide * wide, axis=1, keepdims=True)
    n = Y * part
    center = jnp.sum(wide.reshape(Z, n, d), axis=1, keepdims=True) * (1.0 / n)
    of_mean = jnp.sum(center * center, axis=2, keepdims=True)
    of_rows = jnp.sum(row_sq.reshape(Z, n, 1), axis=1, keepdims=True) * (1.0 / n)
    noise = (of_rows - of_mean) * (1.0 / (n - 1))
    center = center * jnp.maximum(1.0 - noise / jnp.maximum(of_mean, 1e-30), 0.0)
    row_sq = row_sq * SCALE

    def less_center(total, mass):
        parted = total.reshape(Z, Y * part, d) - mass.reshape(Z, Y * part, 1) * center
        return parted.reshape(half, d)

    got_cols = slots(cols, 0, 2 * n_grp - 1, col_send, col_recv)
    got_cols.wait_recv()
    cmat = cols[...].astype(jnp.float32).reshape(2 * n_grp * part, d).astype(jnp.bfloat16)
    cturn, col_sq = turned(cmat)

    s = (dot(pmat[...], cturn) * 2.0 - col_sq) * SCALE
    s = jnp.where(same, MASKED, s)
    s_top = jnp.max(s, axis=1, keepdims=True)
    w = jnp.where(same, 0.0, jnp.exp2(s - s_top))
    s_mass = jnp.sum(w, axis=1, keepdims=True)
    s_sum = dot(w.astype(jnp.bfloat16), cmat)
    send_s[...] = less_center(s_sum, s_mass).reshape(chips, part, d).astype(jnp.bfloat16)


    top = jnp.full((half, LANES), -jnp.inf, jnp.float32)
    for j in range(2 * chunks):
        if j == 2 * chunks - LATE:
            for a, b in far_first:
                where, slot = returns_to(a, b)
                remote(send_s.at[a * Y + b], recv_s.at[slot], s_send, s_recv, **where).start()
            recv_s[0] = send_s[0]
        if j >= 2 * chunks - LATE:
            pass_on(j - chunks).wait_recv()
            take(j)
        s = dot(pmat[...], turn[j]) * (2.0 * SCALE) - ref_sq[j]
        scores[j] = s
        for at in range(0, CHUNK, LANES):
            top = jnp.maximum(top, s[:, at : at + LANES])
    top = jnp.max(top, axis=1, keepdims=True)
    mass = jnp.zeros((half, LANES), jnp.float32)
    for j in range(2 * chunks):
        w = jnp.exp2(scores[j] - top)
        for at in range(0, CHUNK, LANES):
            mass = mass + w[:, at : at + LANES]
        term = dot(w.astype(jnp.bfloat16), smp[j])
        if j == 0:
            acc[...] = term
        else:
            acc[...] += term
    mass = jnp.sum(mass, axis=1, keepdims=True)
    send_t[...] = packed(part, top - row_sq, mass, s_top - row_sq, s_mass)
    for a, b in far_first:
        where, slot = returns_to(a, b)
        remote(send_t.at[a * Y + b], recv_t.at[slot], t_send, t_recv, **where).start()
    recv_t[0] = send_t[0]
    total = less_center(acc[...], mass)
    send_c[...] = total.reshape(chips, part, d).astype(jnp.bfloat16)

    for a, b in far_first:
        where, slot = returns_to(a, b)
        remote(send_c.at[a * Y + b], recv_c.at[slot], c_send, c_recv, **where).start()
    recv_c[0] = send_c[0]

    got_s = slots(recv_s, 0, chips - 1, s_send, s_recv)
    got_c = slots(recv_c, 0, chips - 1, c_send, c_recv)
    got_t = slots(recv_t, 0, chips - 1, t_send, t_recv)
    got_s.wait_recv()
    got_t.wait_recv()
    c_top, c_mass, s_top, s_mass = unpacked(recv_t[...], part, 4)
    wide = p_ref[...].astype(jnp.float32)
    s_share = shares(s_top, s_mass) * STEP_SIZE
    c_share = jnp.broadcast_to(shares(c_top, c_mass) * STEP_SIZE, (chips, part, LANES))
    out_ref[...] = wide - jnp.sum(s_share * recv_s[...].astype(jnp.float32), axis=0)
    got_c.wait_recv()
    for at in range(0, d, LANES):
        lanes = pl.ds(at, LANES)
        out_ref[:, lanes] += jnp.sum(c_share * recv_c[:, :, lanes].astype(jnp.float32), axis=0)
    got_rows.wait_send()
    got_cols.wait_send()
    slots(smp, 0, chunks, smp_send, smp_recv.at[0]).wait_send()
    got_s.wait_send()
    got_c.wait_send()
    got_t.wait_send()


def per_device(n_ref, n_grp, particles, samples):
    part, d = particles.shape
    refs = samples.shape[0]
    chips, chunks = n_ref // 2, refs // CHUNK
    half = chips * part
    dma = pltpu.SemaphoreType.DMA
    bf16, f32 = jnp.bfloat16, jnp.float32
    return pl.pallas_call(
        kernel,
        out_shape=pltpu.VMEM((part, d), f32),
        in_specs=[pl.BlockSpec(memory_space=pl.ANY)] * 2,
        out_specs=pl.BlockSpec(memory_space=pltpu.VMEM),
        scratch_shapes=[
            pltpu.VMEM((part, d), bf16),
            pltpu.VMEM((2 * chunks, CHUNK, d), bf16),
            pltpu.VMEM((2 * chunks, d, CHUNK), bf16),
            pltpu.VMEM((chips, part, d), bf16),
            pltpu.VMEM((2 * n_grp, part, d), bf16),
            pltpu.VMEM((half, d), bf16),
            pltpu.VMEM((2 * chunks, 1, CHUNK), f32),
            pltpu.VMEM((2 * chunks, half, CHUNK), f32),
            pltpu.VMEM((half, d), f32),
            pltpu.VMEM((chips, part, d), bf16),
            pltpu.VMEM((chips, part, d), bf16),
            pltpu.VMEM((chips, part, d), bf16),
            pltpu.VMEM((chips, part, d), bf16),
            pltpu.VMEM((chips, 1, LANES), f32),
            pltpu.VMEM((chips, 1, LANES), f32),
            dma((chunks,)), dma, dma, dma, dma, dma, dma, dma((chunks,)),
            dma, dma, dma, dma, dma, dma,
        ],
        compiler_params=pltpu.CompilerParams(
            collective_id=0, has_side_effects=True, vmem_limit_bytes=VMEM_BYTES
        ),
        name="mmd_step",
    )(particles, samples)


def solution(mesh):
    step = functools.partial(per_device, mesh.shape["ref"], mesh.shape["grp"])
    return jax.shard_map(
        step,
        mesh=mesh,
        in_specs=(P(("grp", "ref"), None), P("ref", None)),
        out_specs=P(("grp", "ref"), None),
        check_vma=False,
    )
```
